32 devices in a mesh: row: 4 (over z), col: 4 (over y, x), leaf: 2 (over core).
Axes of the slice: x: 2, y: 2, z: 4, core: 2. Of those that a mesh axis runs over, the one named last changes fastest.
Arguments:
- separator: float32 [8192, 16384], P('row', 'col'), may hold values from -6 to 6
- col_panels: bfloat16 [2, 8192, 1536], P('leaf', 'row', 'col'), may hold values from -0.15625 to 0.15625
- row_panels: bfloat16 [2, 1536, 16384], P('leaf', 'row', 'col'), may hold values from -6 to 6
- rows_list: int32 [2, 6, 16], replicated, may hold values from 0 to 63
- cols_list: int32 [2, 6, 32], replicated, may hold values from 0 to 127
- inverses: float32 [8192, 256], P('row'), may hold values from -0.375 to 0.375
Outputs:
- solved: float32 [8192, 16384], P('row', ('col', 'leaf'))
The draws below stay inside these ranges and needn't reach their ends.
All inputs are finite; a program needn't handle non-finite values.
Results may differ from the reference program's by a relative error of at most 0.0003.
Values may be sent and summed in bfloat16 or wider, within the bound.
A program may use at most 192 MiB of HBM per device.

```python
import jax
import jax.numpy as jnp
from jax import lax

NS = 8192
W = 256
K = 6
BLK = 128
RB = 16
CB = 32
NCOLS = 16384
KW = 1536


def with_ends(drawn, rng, least, top_value):
    spot = [jax.random.randint(jax.random.fold_in(rng, axis), (), 0, length) for axis, length in enumerate(drawn.shape)]
    longest = drawn.shape.index(max(drawn.shape))
    neighbour = spot[:longest] + [(spot[longest] + 1) % drawn.shape[longest]] + spot[longest + 1:]
    return drawn.at[tuple(spot)].set(least).at[tuple(neighbour)].set(top_value)


def levels(key, extent, split, low, largest):
    gain = 1.0
    for axis_at, blocks in split:
        steps = jax.random.uniform(jax.random.fold_in(jax.random.fold_in(key, 6), axis_at), (blocks,), jnp.float32, low / len(split), largest / len(split))
        gain = gain * jnp.repeat(jnp.exp(steps), extent[axis_at] // blocks).reshape((-1,) + (1,) * (len(extent) - 1 - axis_at))
    return gain


def normal_values(rng, extent, spread, limit, pieces=(), held_as=jnp.bfloat16):
    array = jax.random.normal(rng, extent, jnp.float32) * spread
    if len(pieces) > 0:
        array = levels(rng, extent, pieces, -0.22, 0.18) * array
    return jnp.clip(array, min=-limit, max=limit).astype(held_as)


def setup_inputs(seed: int = 0) -> dict:
    key_list = jax.random.split(jax.random.key(seed), 7)
    separator = normal_values(key_list[0], (NS, NCOLS), 1.0, 6.0, ((0, 4), (1, 4)), jnp.float32)
    col_panels = normal_values(key_list[1], (2, NS, KW), KW ** -0.5, 0.15625, ((0, 2), (1, 4), (2, 4)))
    row_panels = normal_values(key_list[2], (2, KW, NCOLS), 1.0, 6.0, ((0, 2), (1, 4), (2, 4)))
    rows_list = with_ends(jax.random.randint(key_list[3], (2, K, RB), 0, NS // BLK), jax.random.fold_in(key_list[3], 1), 0, (NS // BLK) - 1).astype(jnp.int32)
    cols_list = with_ends(jax.random.randint(key_list[4], (2, K, CB), 0, NCOLS // BLK), jax.random.fold_in(key_list[4], 1), 0, (NCOLS // BLK) - 1).astype(jnp.int32)
    inverses = normal_values(key_list[5], (NS, W), W ** -0.5, 0.375, ((0, 4),), jnp.float32)
    return {"separator": separator, "col_panels": col_panels, "row_panels": row_panels, "rows_list": rows_list, "cols_list": cols_list, "inverses": inverses}


def subtree_update(lower_raw, upper_raw, row_list, col_list):
    row_block = jnp.arange(NS, dtype=jnp.int32) // BLK
    col_block = jnp.arange(NCOLS, dtype=jnp.int32) // BLK
    row_mask = jnp.any(row_list[:, :, None] == row_block[None, None, :], axis=1)
    col_mask = jnp.any(col_list[:, :, None] == col_block[None, None, :], axis=1)
    owner = jnp.arange(KW, dtype=jnp.int32) // W
    lower = jnp.where(row_mask[owner].T, lower_raw, jnp.zeros_like(lower_raw))
    upper = jnp.where(col_mask[owner], upper_raw, jnp.zeros_like(upper_raw))
    return jnp.dot(lower, upper, preferred_element_type=jnp.float32)


def reference(separator, col_panels, row_panels, rows_list, cols_list, inverses):
    combined = separator - subtree_update(col_panels[0], row_panels[0], rows_list[0], cols_list[0])
    combined = combined - subtree_update(col_panels[1], row_panels[1], rows_list[1], cols_list[1])
    blocks = combined.reshape(NS // W, W, NCOLS)
    factor = inverses.reshape(NS // W, W, W)
    solved = jnp.einsum("bij,bjc->bic", factor, blocks, precision=lax.Precision.HIGHEST)
    return solved.reshape(NS, NCOLS)
```

```python
import functools

import jax
import jax.numpy as jnp
from jax import lax
from jax.experimental import pallas as pl
from jax.experimental.pallas import tpu as pltpu
from jax.sharding import PartitionSpec as P

W = 256
BLK = 128
MESH = pl.DeviceIdType.MESH


def touched(index_list, positions):
    return jnp.any(index_list[:, :, :, None] == (positions // BLK)[None, None, None, :], axis=2)


def dense_device(separator, col_panels, row_panels, rows_list, cols_list, inverses):
    loc_rows = separator.shape[0]
    loc_cols = separator.shape[1]
    half = loc_cols // 2
    mine = lax.axis_index("leaf")
    row_ids = lax.axis_index("row") * loc_rows + jnp.arange(loc_rows, dtype=jnp.int32)
    subtrees = jnp.stack([mine])
    col_ids = lax.axis_index("col") * loc_cols + jnp.arange(loc_cols, dtype=jnp.int32)
    row_mask = touched(jnp.take(rows_list, subtrees, axis=0), row_ids)
    col_mask = touched(jnp.take(cols_list, subtrees, axis=0), col_ids)
    upper_all = lax.all_gather(row_panels, "row", axis=1, tiled=True)
    owner_all = jnp.arange(upper_all.shape[1], dtype=jnp.int32) // W
    keep_upper = jnp.take(col_mask, owner_all, axis=1)
    upper_all = jnp.where(keep_upper, upper_all, jnp.zeros_like(upper_all))
    piece = lax.all_gather(col_panels, "col", axis=2, tiled=True)
    owner = jnp.arange(piece.shape[2], dtype=jnp.int32) // W
    keep_lower = jnp.transpose(jnp.take(row_mask, owner, axis=1), (0, 2, 1))
    masked = jnp.where(keep_lower, piece, jnp.zeros_like(piece))
    update = jnp.einsum("srj,sjc->rc", masked, upper_all, preferred_element_type=jnp.float32)
    own_part = lax.dynamic_slice_in_dim(separator, mine * half, half, 1)
    both = lax.psum_scatter(update, "leaf", scatter_dimension=1, tiled=True)
    combined = own_part - both
    blocks = combined.reshape(loc_rows // W, W, half)
    factor = inverses.reshape(loc_rows // W, W, W)
    solved = jnp.einsum("bij,bjc->bic", factor, blocks, precision=lax.Precision.HIGHEST)
    return solved.reshape(loc_rows, half)


def pack_kernel(n_row, n_col, tr, tc, hb, nb, tab, own, other, col, pu, pc):
    base_l = n_row * 2 * tr * hb
    base_i = base_l + 2 * n_col * tc * nb
    r, c, mine = tab[base_i], tab[base_i + 1], tab[base_i + 2]
    for src, leaf in ((own, mine), (other, 1 - mine)):
        for t in range(tr):
            @pl.loop(0, hb)
            def _(j, src=src, leaf=leaf, t=t):
                p = tab[((r * 2 + leaf) * tr + t) * hb + j]

                @pl.when(p >= 0)
                def _():
                    at = pl.ds(pl.multiple_of(j * BLK, BLK), BLK)
                    pu[p] = src[0, pl.ds(t * BLK, BLK), at]
    for t in range(tc):
        @pl.loop(0, nb)
        def _(i, t=t):
            p = tab[base_l + ((mine * n_col + c) * tc + t) * nb + i]

            @pl.when(p >= 0)
            def _():
                at = pl.ds(pl.multiple_of(i * BLK, BLK), BLK)
                pc[p] = col[0, at, pl.ds(t * BLK, BLK)]


def comm_kernel(n_row, n_col, cap_u, cap_l, pu, pc, gu, gc, su, ru, sl, rl, sf, rf):
    r, c, mine = lax.axis_index("row"), lax.axis_index("col"), lax.axis_index("leaf")
    nu, nl = pl.ds(0, cap_u), pl.ds(0, cap_l)
    barrier = pltpu.get_barrier_semaphore()
    for d in (1, n_row - 1):
        pl.semaphore_signal(barrier, inc=1, device_id={"row": lax.rem(r + d, n_row)}, device_id_type=MESH)
    for d in range(1, n_col):
        pl.semaphore_signal(barrier, inc=1, device_id={"col": lax.rem(c + d, n_col)}, device_id_type=MESH)
    pl.semaphore_signal(barrier, inc=1, device_id={"leaf": 1 - mine}, device_id_type=MESH)
    pl.semaphore_wait(barrier, n_col + 2)

    def line(way, step, shard, target, first):
        src = pu.at[nu] if first else gu.at[shard, nu]
        return pltpu.make_async_remote_copy(
            src_ref=src, dst_ref=gu.at[shard, nu], send_sem=su.at[way, step], recv_sem=ru.at[way, step],
            device_id={"row": target}, device_id_type=MESH)

    def line_sends(step, act):
        @pl.when(jnp.logical_and(r >= 1, r + step <= n_row - 1))
        def _():
            act(line(0, step, r + step, r - 1, step == 0))

        @pl.when(jnp.logical_and(r <= n_row - 2, r >= step))
        def _():
            act(line(1, step, r - step, r + 1, step == 0))

    def line_waits(step):
        @pl.when(r + 1 + step <= n_row - 1)
        def _():
            line(0, step, r + 1 + step, r + 1, False).wait_recv()

        @pl.when(r >= 1 + step)
        def _():
            line(1, step, r - 1 - step, r - 1, False).wait_recv()

    def across(d):
        return pltpu.make_async_remote_copy(
            src_ref=pc.at[nl], dst_ref=gc.at[mine * n_col + c, nl], send_sem=sl.at[d], recv_sem=rl.at[d],
            device_id={"col": lax.rem(c + d, n_col)}, device_id_type=MESH)

    def arrived(d):
        slot = mine * n_col + lax.rem(c + n_col - d, n_col)
        return pltpu.make_async_remote_copy(
            src_ref=pc.at[nl], dst_ref=gc.at[slot, nl], send_sem=sl.at[d], recv_sem=rl.at[d],
            device_id={"col": lax.rem(c + d, n_col)}, device_id_type=MESH)

    def pair(d, leaf):
        slot = leaf * n_col + lax.rem(c + n_col - d, n_col)
        return pltpu.make_async_remote_copy(
            src_ref=pc.at[nl] if d == 0 else gc.at[slot, nl], dst_ref=gc.at[slot, nl],
            send_sem=sf.at[d], recv_sem=rf.at[d], device_id={"leaf": 1 - mine}, device_id_type=MESH)

    line_sends(0, lambda copy: copy.start())
    for d in range(1, n_col):
        across(d).start()
    pair(0, mine).start()
    for step in range(n_row - 1):
        if step > 0:
            line_sends(step, lambda copy: copy.start())
        if step == min(1, n_row - 2):
            for d in range(1, n_col):
                arrived(d).wait_recv()
                pair(d, mine).start()
        line_waits(step)
    for d in range(n_col):
        pair(d, 1 - mine).wait_recv()
    for d in range(n_col):
        pair(d, mine).wait_send()
    for d in range(1, n_col):
        across(d).wait_send()
    for step in range(n_row - 1):
        line_sends(step, lambda copy: copy.wait_send())


def split(x):
    hi = x.astype(jnp.bfloat16)
    return hi, (x - hi.astype(jnp.float32)).astype(jnp.bfloat16)


def solve_kernel(n_row, n_col, tr, tc, hb, nb, kk, tile, tab, sep, inv, pu, pc, gu, gc, out, low, up, acc, sem):
    base_l = n_row * 2 * tr * hb
    base_i = base_l + 2 * n_col * tc * nb
    sw = W // BLK
    b = pl.program_id(0)

    def at_u(leaf, k, q):
        s = k * sw + q
        return (((s // tr) * 2 + leaf) * tr + s % tr) * hb

    def at_l(leaf, k, q):
        return base_l + (leaf * kk * sw + k * sw + q) * nb

    @pl.when(b == 0)
    def _():
        r, c, mine, total = tab[base_i], tab[base_i + 1], tab[base_i + 2], tab[base_i + 3]

        @pl.loop(0, 2 * kk)
        def _(m):
            low[m] = jnp.zeros(low.shape[1:], low.dtype)
            up[m] = jnp.zeros(up.shape[1:], up.dtype)

        for leaf in range(2):
            for k in range(kk):
                @pl.loop(0, hb)
                def _(j, leaf=leaf, k=k):
                    @pl.when(tab[at_u(leaf, k, 0) + j] >= 0)
                    def _():
                        at = pl.ds(pl.multiple_of(j * BLK, BLK), BLK)
                        for q in range(sw):
                            p = tab[at_u(leaf, k, q) + j]
                            owner = (k * sw + q) // tr
                            dst = up.at[leaf * kk + k, pl.ds(q * BLK, BLK), at]

                            @pl.when(owner == r)
                            def _():
                                pltpu.make_async_copy(pu.at[p], dst, sem).start()

                            @pl.when(owner != r)
                            def _():
                                pltpu.make_async_copy(gu.at[owner, p], dst, sem).start()

                @pl.loop(0, nb)
                def _(i, leaf=leaf, k=k):
                    @pl.when(tab[at_l(leaf, k, 0) + i] >= 0)
                    def _():
                        at = pl.ds(pl.multiple_of(i * BLK, BLK), BLK)
                        for q in range(sw):
                            p = tab[at_l(leaf, k, q) + i]
                            owner = (k * sw + q) // tc
                            here = jnp.logical_and(owner == c, leaf == mine)
                            dst = low.at[leaf * kk + k, at, pl.ds(q * BLK, BLK)]

                            @pl.when(here)
                            def _():
                                pltpu.make_async_copy(pc.at[p], dst, sem).start()

                            @pl.when(jnp.logical_not(here))
                            def _():
                                pltpu.make_async_copy(gc.at[leaf * n_col + owner, p], dst, sem).start()

        @pl.loop(0, total)
        def _(n):
            pltpu.make_async_copy(pc.at[0], low.at[0, pl.ds(0, BLK), pl.ds(0, BLK)], sem).wait()

    acc[...] = sep[...]
    cols = out.shape[1]
    rows = pl.ds(pl.multiple_of(b * W, W), W)
    per = tile // BLK
    for leaf in range(2):
        for k in range(kk):
            hit = tab[at_l(leaf, k, 0) + b * sw]
            for q in range(1, sw):
                hit = jnp.maximum(hit, tab[at_l(leaf, k, 0) + b * sw + q])

            @pl.when(hit >= 0)
            def _(leaf=leaf, k=k):
                for n in range(cols // tile):
                    col_hit = tab[at_u(leaf, k, 0) + n * per]
                    for q in range(1, per):
                        col_hit = jnp.maximum(col_hit, tab[at_u(leaf, k, 0) + n * per + q])

                    @pl.when(col_hit >= 0)
                    def _(n=n):
                        at = pl.ds(n * tile, tile)
                        acc[:, at] -= jnp.dot(low[leaf * kk + k, rows, :], up[leaf * kk + k, :, at],
                                              preferred_element_type=jnp.float32)
    f_hi, f_lo = split(inv[...])
    for n in range(cols // tile):
        at = pl.ds(n * tile, tile)
        hi, lo = split(acc[:, at])
        out[:, at] = (jnp.dot(f_hi, hi, preferred_element_type=jnp.float32)
                      + (jnp.dot(f_hi, lo, preferred_element_type=jnp.float32)
                         + jnp.dot(f_lo, hi, preferred_element_type=jnp.float32)))


def caps(full, fractions):
    return [max(1, -(-full * f // 96)) for f in fractions] + [full]


def sparse_device(n_row, n_col, separator, col_panels, row_panels, rows_list, cols_list, inverses):
    loc_rows, loc_cols = separator.shape
    half = loc_cols // 2
    tr, tc = row_panels.shape[1] // BLK, col_panels.shape[2] // BLK
    hb, nb = half // BLK, loc_rows // BLK
    kk = rows_list.shape[1]
    sw = W // BLK
    full_u, full_l = 2 * tr * hb, tc * nb
    r, c, mine = lax.axis_index("row"), lax.axis_index("col"), lax.axis_index("leaf")

    away = lax.dynamic_slice_in_dim(row_panels, (1 - mine) * half, half, 2)
    other = lax.ppermute(away, "leaf", [(0, 1), (1, 0)])

    def slices(mask, lead):
        return jnp.broadcast_to(mask[:, :, None], (2, kk, sw) + mask.shape[2:]).reshape((2, lead, -1) + mask.shape[2:])

    def places(mask):
        n = mask.shape[1]
        before = (jnp.arange(n)[:, None] < jnp.arange(n)[None, :]).astype(jnp.bfloat16)
        at = jnp.dot(mask.astype(jnp.bfloat16), before, preferred_element_type=jnp.float32).astype(jnp.int32)
        return jnp.where(mask, at, -1).reshape(-1)

    def named(index_list, ids):
        return jnp.any(index_list[:, :, :, None] == ids, axis=2)

    mine_u = named(cols_list, (c * 2 + mine) * hb + jnp.arange(hb, dtype=jnp.int32))
    mine_u = jnp.transpose(slices(mine_u, n_row), (1, 0, 2, 3)).reshape(n_row, full_u)
    mine_l = named(rows_list, r * nb + jnp.arange(nb, dtype=jnp.int32))
    mine_l = slices(mine_l, n_col).reshape(2 * n_col, full_l)
    total = jnp.sum(mine_u, dtype=jnp.int32) + jnp.sum(mine_l, dtype=jnp.int32)
    tab = jnp.concatenate([places(mine_u), places(mine_l), jnp.stack([r, c, mine, total]).astype(jnp.int32)])

    all_u = named(cols_list, jnp.arange(n_col * 2 * hb, dtype=jnp.int32)).reshape(2, kk, n_col * 2, hb)
    most_u = jnp.max(jnp.sum(slices(all_u, n_row), axis=(0, 2, 4), dtype=jnp.int32))
    all_l = named(rows_list, jnp.arange(n_row * nb, dtype=jnp.int32)).reshape(2, kk, n_row, nb)
    most_l = jnp.max(jnp.sum(slices(all_l, n_col), axis=(2, 4), dtype=jnp.int32))
    caps_u = caps(full_u, (28, 32, 36, 42, 56))
    caps_l = caps(full_l, (44, 44, 48, 52, 60))
    level = jnp.maximum(sum((most_u > x).astype(jnp.int32) for x in caps_u[:-1]),
                        sum((most_l > x).astype(jnp.int32) for x in caps_l[:-1]))

    block = (BLK, BLK)
    bf16 = jnp.bfloat16
    pu, pc = pl.pallas_call(
        functools.partial(pack_kernel, n_row, n_col, tr, tc, hb, nb),
        out_shape=(jax.ShapeDtypeStruct((full_u,) + block, bf16), jax.ShapeDtypeStruct((full_l,) + block, bf16)),
        grid_spec=pltpu.PrefetchScalarGridSpec(
            num_scalar_prefetch=1, grid=(1,),
            in_specs=[
                pl.BlockSpec((1, tr * BLK, half), lambda i, t: (0, 0, t[t.shape[0] - 2])),
                pl.BlockSpec((1, tr * BLK, half), lambda i, t: (0, 0, 0)),
                pl.BlockSpec((1, loc_rows, tc * BLK), lambda i, t: (0, 0, 0)),
            ],
            out_specs=[pl.BlockSpec((full_u,) + block, lambda i, t: (0, 0, 0)),
                       pl.BlockSpec((full_l,) + block, lambda i, t: (0, 0, 0))]),
        compiler_params=pltpu.CompilerParams(vmem_limit_bytes=40 * 2**20),
    )(tab, row_panels, other, col_panels)

    hbm = pl.BlockSpec(memory_space=pl.ANY)
    dma = pltpu.SemaphoreType.DMA

    def exchange(which):
        def run(a, b):
            return pl.pallas_call(
                functools.partial(comm_kernel, n_row, n_col, caps_u[which], caps_l[which]),
                out_shape=(jax.ShapeDtypeStruct((n_row, full_u) + block, bf16),
                           jax.ShapeDtypeStruct((2 * n_col, full_l) + block, bf16)),
                in_specs=[hbm, hbm], out_specs=(hbm, hbm),
                scratch_shapes=[dma((2, n_row)), dma((2, n_row))] + [dma((n_col,))] * 4,
                compiler_params=pltpu.CompilerParams(collective_id=which, has_side_effects=True),
                name="exchange%d" % which,
            )(a, b)
        return run

    gu, gc = lax.switch(level, [exchange(i) for i in range(len(caps_u))], pu, pc)

    tile = min(512, half)
    return pl.pallas_call(
        functools.partial(solve_kernel, n_row, n_col, tr, tc, hb, nb, kk, tile),
        out_shape=jax.ShapeDtypeStruct((loc_rows, half), jnp.float32),
        grid_spec=pltpu.PrefetchScalarGridSpec(
            num_scalar_prefetch=1, grid=(loc_rows // W,),
            in_specs=[pl.BlockSpec((W, half), lambda i, t: (i, t[t.shape[0] - 2])),
                      pl.BlockSpec((W, W), lambda i, t: (i, 0)), hbm, hbm, hbm, hbm],
            out_specs=pl.BlockSpec((W, half), lambda i, t: (i, 0)),
            scratch_shapes=[pltpu.VMEM((2 * kk, loc_rows, W), bf16), pltpu.VMEM((2 * kk, W, half), bf16),
                            pltpu.VMEM((W, half), jnp.float32), dma]),
        compiler_params=pltpu.CompilerParams(vmem_limit_bytes=56 * 2**20),
    )(tab, separator, inverses, pu, pc, gu, gc)


def solution(mesh):
    placed = (
        P("row", "col"),
        P("leaf", "row", "col"),
        P("leaf", "row", "col"),
        P(),
        P(),
        P("row", None),
    )
    n_row, n_col = mesh.shape["row"], mesh.shape["col"]

    def per_device(separator, col_panels, row_panels, *rest):
        whole = separator.shape[1] % (2 * W) == 0 and separator.shape[0] % W == 0
        if whole and row_panels.shape[1] % BLK == 0 and col_panels.shape[2] % BLK == 0 and mesh.shape["leaf"] == 2:
            return sparse_device(n_row, n_col, separator, col_panels, row_panels, *rest)
        return dense_device(separator, col_panels, row_panels, *rest)

    return jax.shard_map(
        per_device, mesh=mesh, in_specs=placed, out_specs=P("row", ("col", "leaf")), check_vma=False
    )
```

```python
import functools

import jax
import jax.numpy as jnp
from jax import lax
from jax.experimental import pallas as pl
from jax.experimental.pallas import tpu as pltpu
from jax.sharding import PartitionSpec as P

W = 256
BLK = 128
MESH = pl.DeviceIdType.MESH


def touched(index_list, positions):
    return jnp.any(index_list[:, :, :, None] == (positions // BLK)[None, None, None, :], axis=2)


def dense_device(separator, col_panels, row_panels, rows_list, cols_list, inverses):
    loc_rows = separator.shape[0]
    loc_cols = separator.shape[1]
    half = loc_cols // 2
    mine = lax.axis_index("leaf")
    row_ids = lax.axis_index("row") * loc_rows + jnp.arange(loc_rows, dtype=jnp.int32)
    subtrees = jnp.stack([mine])
    col_ids = lax.axis_index("col") * loc_cols + jnp.arange(loc_cols, dtype=jnp.int32)
    row_mask = touched(jnp.take(rows_list, subtrees, axis=0), row_ids)
    col_mask = touched(jnp.take(cols_list, subtrees, axis=0), col_ids)
    upper_all = lax.all_gather(row_panels, "row", axis=1, tiled=True)
    owner_all = jnp.arange(upper_all.shape[1], dtype=jnp.int32) // W
    keep_upper = jnp.take(col_mask, owner_all, axis=1)
    upper_all = jnp.where(keep_upper, upper_all, jnp.zeros_like(upper_all))
    piece = lax.all_gather(col_panels, "col", axis=2, tiled=True)
    owner = jnp.arange(piece.shape[2], dtype=jnp.int32) // W
    keep_lower = jnp.transpose(jnp.take(row_mask, owner, axis=1), (0, 2, 1))
    masked = jnp.where(keep_lower, piece, jnp.zeros_like(piece))
    update = jnp.einsum("srj,sjc->rc", masked, upper_all, preferred_element_type=jnp.float32)
    own_part = lax.dynamic_slice_in_dim(separator, mine * half, half, 1)
    both = lax.psum_scatter(update, "leaf", scatter_dimension=1, tiled=True)
    combined = own_part - both
    blocks = combined.reshape(loc_rows // W, W, half)
    factor = inverses.reshape(loc_rows // W, W, W)
    solved = jnp.einsum("bij,bjc->bic", factor, blocks, precision=lax.Precision.HIGHEST)
    return solved.reshape(loc_rows, half)


def pack_kernel(n_row, n_col, tr, tc, hb, nb, kk, caps_u, caps_l, tab, own, other, col, pu, pc, level):
    base_l = n_row * 2 * tr * hb
    base_i = base_l + 2 * n_col * tc * nb
    r, c, mine = tab[base_i], tab[base_i + 1], tab[base_i + 2]
    sw = W // BLK
    base_u, halves = base_i + 3, 2 * n_col
    base_r = base_u + 2 * kk * halves

    def most_in_rows(h, most):
        for x in range(n_row):
            parts = [tab[base_u + (leaf * kk + (x * tr + t) // sw) * halves + h] for leaf in range(2) for t in range(tr)]
            most = jnp.maximum(most, sum(parts[1:], parts[0]))
        return most

    def most_in_cols(h, most):
        for leaf in range(2):
            for x in range(n_col):
                parts = [tab[base_r + (leaf * kk + (x * tc + t) // sw) * n_row + h] for t in range(tc)]
                most = jnp.maximum(most, sum(parts[1:], parts[0]))
        return most

    most_u = lax.fori_loop(0, halves, most_in_rows, jnp.int32(0))
    most_l = lax.fori_loop(0, n_row, most_in_cols, jnp.int32(0))
    over = jnp.int32(0)
    for cap_u, cap_l in zip(caps_u[:-1], caps_l[:-1]):
        over = over + jnp.logical_or(most_u > cap_u, most_l > cap_l).astype(jnp.int32)
    level[0] = over

    for src, leaf in ((own, mine), (other, 1 - mine)):
        for t in range(tr):
            @pl.loop(0, hb)
            def _(j, src=src, leaf=leaf, t=t):
                p = tab[((r * 2 + leaf) * tr + t) * hb + j]

                @pl.when(p >= 0)
                def _():
                    at = pl.ds(pl.multiple_of(j * BLK, BLK), BLK)
                    pu[p] = src[0, pl.ds(t * BLK, BLK), at]
    for t in range(tc):
        @pl.loop(0, nb)
        def _(i, t=t):
            p = tab[base_l + ((mine * n_col + c) * tc + t) * nb + i]

            @pl.when(p >= 0)
            def _():
                at = pl.ds(pl.multiple_of(i * BLK, BLK), BLK)
                pc[p] = col[0, at, pl.ds(t * BLK, BLK)]


def comm_kernel(n_row, n_col, cap_u, cap_l, pu, pc, gu, gc, su, ru, sl, rl, sf, rf):
    r, c, mine = lax.axis_index("row"), lax.axis_index("col"), lax.axis_index("leaf")
    nu, nl = pl.ds(0, cap_u), pl.ds(0, cap_l)
    barrier = pltpu.get_barrier_semaphore()
    for d in (1, n_row - 1):
        pl.semaphore_signal(barrier, inc=1, device_id={"row": lax.rem(r + d, n_row)}, device_id_type=MESH)
    for d in range(1, n_col):
        pl.semaphore_signal(barrier, inc=1, device_id={"col": lax.rem(c + d, n_col)}, device_id_type=MESH)
    pl.semaphore_signal(barrier, inc=1, device_id={"leaf": 1 - mine}, device_id_type=MESH)
    pl.semaphore_wait(barrier, n_col + 2)

    def line(way, step, shard, target, first):
        src = pu.at[nu] if first else gu.at[shard, nu]
        return pltpu.make_async_remote_copy(
            src_ref=src, dst_ref=gu.at[shard, nu], send_sem=su.at[way, step], recv_sem=ru.at[way, step],
            device_id={"row": target}, device_id_type=MESH)

    def line_sends(step, act):
        @pl.when(jnp.logical_and(r >= 1, r + step <= n_row - 1))
        def _():
            act(line(0, step, r + step, r - 1, step == 0))

        @pl.when(jnp.logical_and(r <= n_row - 2, r >= step))
        def _():
            act(line(1, step, r - step, r + 1, step == 0))

    def line_waits(step):
        @pl.when(r + 1 + step <= n_row - 1)
        def _():
            line(0, step, r + 1 + step, r + 1, False).wait_recv()

        @pl.when(r >= 1 + step)
        def _():
            line(1, step, r - 1 - step, r - 1, False).wait_recv()

    def across(d):
        return pltpu.make_async_remote_copy(
            src_ref=pc.at[nl], dst_ref=gc.at[mine * n_col + c, nl], send_sem=sl.at[d], recv_sem=rl.at[d],
            device_id={"col": lax.rem(c + d, n_col)}, device_id_type=MESH)

    def arrived(d):
        slot = mine * n_col + lax.rem(c + n_col - d, n_col)
        return pltpu.make_async_remote_copy(
            src_ref=pc.at[nl], dst_ref=gc.at[slot, nl], send_sem=sl.at[d], recv_sem=rl.at[d],
            device_id={"col": lax.rem(c + d, n_col)}, device_id_type=MESH)

    def pair(d, leaf):
        slot = leaf * n_col + lax.rem(c + n_col - d, n_col)
        return pltpu.make_async_remote_copy(
            src_ref=pc.at[nl] if d == 0 else gc.at[slot, nl], dst_ref=gc.at[slot, nl],
            send_sem=sf.at[d], recv_sem=rf.at[d], device_id={"leaf": 1 - mine}, device_id_type=MESH)

    line_sends(0, lambda copy: copy.start())
    for d in range(1, n_col):
        across(d).start()
    pair(0, mine).start()
    for step in range(n_row - 1):
        if step > 0:
            line_sends(step, lambda copy: copy.start())
        if step == min(1, n_row - 2):
            for d in range(1, n_col):
                arrived(d).wait_recv()
                pair(d, mine).start()
        line_waits(step)
    for d in range(n_col):
        pair(d, 1 - mine).wait_recv()
    for d in range(n_col):
        pair(d, mine).wait_send()
    for d in range(1, n_col):
        across(d).wait_send()
    for step in range(n_row - 1):
        line_sends(step, lambda copy: copy.wait_send())


def split(x):
    hi = x.astype(jnp.bfloat16)
    return hi, (x - hi.astype(jnp.float32)).astype(jnp.bfloat16)


GROUP = 4


def solve_kernel(n_row, n_col, tr, tc, hb, nb, kk, tab, sep, inv, pu, pc, gu, gc, out,
                 low, up, acc, prod, row_at, col_at, sem, sep_sem):
    base_l = n_row * 2 * tr * hb
    base_i = base_l + 2 * n_col * tc * nb
    sw = W // BLK
    half, loc_rows = hb * BLK, nb * BLK
    b = pl.program_id(0)

    def at_u(leaf, k, q):
        s = k * sw + q
        return (((s // tr) * 2 + leaf) * tr + s % tr) * hb

    def at_l(leaf, k, q):
        return base_l + (leaf * kk * sw + k * sw + q) * nb

    @pl.when(b == 0)
    def _():
        r, c, mine = tab[base_i], tab[base_i + 1], tab[base_i + 2]
        load = pltpu.make_async_copy(
            sep.at[:, pl.ds(pl.multiple_of(mine * half, half), half)],
            acc.at[pl.ds(0, loc_rows), pl.ds(0, half)], sep_sem)
        load.start()
        counts = []
        total = jnp.int32(0)
        for leaf in range(2):
            for k in range(kk):
                m = leaf * kk + k

                def take_col(j, n, leaf=leaf, k=k, m=m):
                    hit = tab[at_u(leaf, k, 0) + j] >= 0

                    @pl.when(hit)
                    def _():
                        col_at[m * (hb + GROUP) + n] = j
                        at = pl.ds(pl.multiple_of(n * BLK, BLK), BLK)
                        for q in range(sw):
                            p = tab[at_u(leaf, k, q) + j]
                            owner = (k * sw + q) // tr
                            dst = up.at[m, pl.ds(q * BLK, BLK), at]

                            @pl.when(owner == r)
                            def _():
                                pltpu.make_async_copy(pu.at[p], dst, sem).start()

                            @pl.when(owner != r)
                            def _():
                                pltpu.make_async_copy(gu.at[owner, p], dst, sem).start()
                    return n + hit.astype(jnp.int32)

                def take_row(i, n, leaf=leaf, k=k, m=m):
                    hit = tab[at_l(leaf, k, 0) + i] >= 0

                    @pl.when(hit)
                    def _():
                        row_at[m * (nb + GROUP) + n] = i
                        at = pl.ds(pl.multiple_of(n * BLK, BLK), BLK)
                        for q in range(sw):
                            p = tab[at_l(leaf, k, q) + i]
                            owner = (k * sw + q) // tc
                            here = jnp.logical_and(owner == c, leaf == mine)
                            dst = low.at[m, at, pl.ds(q * BLK, BLK)]

                            @pl.when(here)
                            def _():
                                pltpu.make_async_copy(pc.at[p], dst, sem).start()

                            @pl.when(jnp.logical_not(here))
                            def _():
                                pltpu.make_async_copy(gc.at[leaf * n_col + owner, p], dst, sem).start()
                    return n + hit.astype(jnp.int32)

                n_u = lax.fori_loop(0, hb, take_col, jnp.int32(0))
                n_l = lax.fori_loop(0, nb, take_row, jnp.int32(0))
                for e in range(GROUP):
                    col_at[m * (hb + GROUP) + n_u + e] = jnp.int32(hb)
                    row_at[m * (nb + GROUP) + n_l + e] = jnp.int32(nb)
                counts.append((n_u, n_l))
                total = total + (n_u + n_l) * sw

        @pl.loop(0, total)
        def _(n):
            pltpu.make_async_copy(pc.at[0], low.at[0, pl.ds(0, BLK), pl.ds(0, BLK)], sem).wait()

        load.wait()
        wide = GROUP * BLK
        for m, (n_u, n_l) in enumerate(counts):
            @pl.loop(0, (n_l + GROUP - 1) // GROUP)
            def _(x, m=m, n_u=n_u, n_l=n_l):
                rows = pl.ds(pl.multiple_of(x * wide, wide), wide)

                @pl.loop(0, (n_u + GROUP - 1) // GROUP)
                def _(y):
                    cols = pl.ds(pl.multiple_of(y * wide, wide), wide)
                    prod[...] = jnp.dot(low[m, rows, :], up[m, :, cols], preferred_element_type=jnp.float32)
                    for i in range(GROUP):
                        row = row_at[m * (nb + GROUP) + x * GROUP + i]

                        @pl.when(row < nb)
                        def _(i=i, row=row):
                            to = pl.ds(pl.multiple_of(row * BLK, BLK), BLK)
                            for j in range(GROUP):
                                col = col_at[m * (hb + GROUP) + y * GROUP + j]
                                at = pl.ds(pl.multiple_of(col * BLK, BLK), BLK)
                                acc[to, at] -= prod[i * BLK:(i + 1) * BLK, j * BLK:(j + 1) * BLK]

    tile = min(512, half)
    rows = pl.ds(pl.multiple_of(b * W, W), W)
    f_hi, f_lo = split(inv[...])
    for n in range(half // tile):
        at = pl.ds(n * tile, tile)
        hi, lo = split(acc[rows, at])
        out[:, at] = (jnp.dot(f_hi, hi, preferred_element_type=jnp.float32)
                      + (jnp.dot(f_hi, lo, preferred_element_type=jnp.float32)
                         + jnp.dot(f_lo, hi, preferred_element_type=jnp.float32)))


def solve_call(n_row, n_col, tr, tc, hb, nb, kk):
    hbm = pl.BlockSpec(memory_space=pl.ANY)
    half, loc_rows = hb * BLK, nb * BLK
    hg, ng = -(-hb // GROUP) * GROUP, -(-nb // GROUP) * GROUP
    return pl.pallas_call(
        functools.partial(solve_kernel, n_row, n_col, tr, tc, hb, nb, kk),
        out_shape=jax.ShapeDtypeStruct((loc_rows, half), jnp.float32),
        grid_spec=pltpu.PrefetchScalarGridSpec(
            num_scalar_prefetch=1, grid=(loc_rows // W,),
            in_specs=[hbm, pl.BlockSpec((W, W), lambda i, t: (i, 0)), hbm, hbm, hbm, hbm],
            out_specs=pl.BlockSpec((W, half), lambda i, t: (i, 0)),
            scratch_shapes=[pltpu.VMEM((2 * kk, ng * BLK, W), jnp.bfloat16),
                            pltpu.VMEM((2 * kk, W, hg * BLK), jnp.bfloat16),
                            pltpu.VMEM((loc_rows, half + BLK), jnp.float32),
                            pltpu.VMEM((GROUP * BLK, GROUP * BLK), jnp.float32),
                            pltpu.SMEM((2 * kk * (nb + GROUP),), jnp.int32),
                            pltpu.SMEM((2 * kk * (hb + GROUP),), jnp.int32),
                            pltpu.SemaphoreType.DMA, pltpu.SemaphoreType.DMA]),
        compiler_params=pltpu.CompilerParams(vmem_limit_bytes=58 * 2**20),
    )


def caps(full, fractions):
    return [max(1, -(-full * f // 96)) for f in fractions] + [full]


def sparse_device(n_row, n_col, separator, col_panels, row_panels, rows_list, cols_list, inverses):
    loc_rows, loc_cols = separator.shape
    half = loc_cols // 2
    tr, tc = row_panels.shape[1] // BLK, col_panels.shape[2] // BLK
    hb, nb = half // BLK, loc_rows // BLK
    kk = rows_list.shape[1]
    sw = W // BLK
    full_u, full_l = 2 * tr * hb, tc * nb
    r, c, mine = lax.axis_index("row"), lax.axis_index("col"), lax.axis_index("leaf")

    away = lax.dynamic_slice_in_dim(row_panels, (1 - mine) * half, half, 2)
    other = lax.ppermute(away, "leaf", [(0, 1), (1, 0)])

    def slices(mask, lead):
        return jnp.broadcast_to(mask[:, :, None], (2, kk, sw) + mask.shape[2:]).reshape((2, lead, -1) + mask.shape[2:])

    def places(mask):
        n = mask.shape[1]
        before = (jnp.arange(n)[:, None] < jnp.arange(n)[None, :]).astype(jnp.bfloat16)
        at = jnp.dot(mask.astype(jnp.bfloat16), before, preferred_element_type=jnp.float32).astype(jnp.int32)
        return jnp.where(mask, at, -1).reshape(-1)

    def named(index_list, ids):
        return jnp.any(index_list[:, :, :, None] == ids, axis=2)

    mine_u = named(cols_list, (c * 2 + mine) * hb + jnp.arange(hb, dtype=jnp.int32))
    mine_u = jnp.transpose(slices(mine_u, n_row), (1, 0, 2, 3)).reshape(n_row, full_u)
    mine_l = named(rows_list, r * nb + jnp.arange(nb, dtype=jnp.int32))
    mine_l = slices(mine_l, n_col).reshape(2 * n_col, full_l)
    all_u = named(cols_list, jnp.arange(n_col * 2 * hb, dtype=jnp.int32)).reshape(2, kk, n_col * 2, hb)
    all_l = named(rows_list, jnp.arange(n_row * nb, dtype=jnp.int32)).reshape(2, kk, n_row, nb)
    tab = jnp.concatenate([
        places(mine_u), places(mine_l), jnp.stack([r, c, mine]).astype(jnp.int32),
        jnp.sum(all_u, axis=3, dtype=jnp.int32).reshape(-1), jnp.sum(all_l, axis=3, dtype=jnp.int32).reshape(-1)])
    caps_u = caps(full_u, (24, 26, 28, 30, 32, 34, 36, 40, 48))
    caps_l = caps(full_l, (40, 44, 44, 44, 48, 48, 48, 52, 60))

    block = (BLK, BLK)
    bf16 = jnp.bfloat16
    at_leaf = n_row * full_u + 2 * n_col * full_l + 2
    pu, pc, level = pl.pallas_call(
        functools.partial(pack_kernel, n_row, n_col, tr, tc, hb, nb, kk, caps_u, caps_l),
        out_shape=(jax.ShapeDtypeStruct((full_u,) + block, bf16), jax.ShapeDtypeStruct((full_l,) + block, bf16),
                   jax.ShapeDtypeStruct((1,), jnp.int32)),
        grid_spec=pltpu.PrefetchScalarGridSpec(
            num_scalar_prefetch=1, grid=(1,),
            in_specs=[
                pl.BlockSpec((1, tr * BLK, half), lambda i, t: (0, 0, t[at_leaf])),
                pl.BlockSpec((1, tr * BLK, half), lambda i, t: (0, 0, 0)),
                pl.BlockSpec((1, loc_rows, tc * BLK), lambda i, t: (0, 0, 0)),
            ],
            out_specs=[pl.BlockSpec((full_u,) + block, lambda i, t: (0, 0, 0)),
                       pl.BlockSpec((full_l,) + block, lambda i, t: (0, 0, 0)),
                       pl.BlockSpec(memory_space=pltpu.SMEM)]),
        compiler_params=pltpu.CompilerParams(vmem_limit_bytes=60 * 2**20),
    )(tab, row_panels, other, col_panels)

    hbm = pl.BlockSpec(memory_space=pl.ANY)
    dma = pltpu.SemaphoreType.DMA

    def exchange(which):
        def run(a, b):
            return pl.pallas_call(
                functools.partial(comm_kernel, n_row, n_col, caps_u[which], caps_l[which]),
                out_shape=(jax.ShapeDtypeStruct((n_row, full_u) + block, bf16),
                           jax.ShapeDtypeStruct((2 * n_col, full_l) + block, bf16)),
                in_specs=[hbm, hbm], out_specs=(hbm, hbm),
                scratch_shapes=[dma((2, n_row)), dma((2, n_row))] + [dma((n_col,))] * 4,
                compiler_params=pltpu.CompilerParams(collective_id=which, has_side_effects=True),
                name="exchange%d" % which,
            )(a, b)
        return run

    gu, gc = lax.switch(level[0], [exchange(i) for i in range(len(caps_u))], pu, pc)

    solve = solve_call(n_row, n_col, tr, tc, hb, nb, kk)
    return solve(tab, separator, inverses, pu, pc, gu, gc)


def solution(mesh):
    placed = (
        P("row", "col"),
        P("leaf", "row", "col"),
        P("leaf", "row", "col"),
        P(),
        P(),
        P("row", None),
    )
    n_row, n_col = mesh.shape["row"], mesh.shape["col"]

    def per_device(separator, col_panels, row_panels, *rest):
        whole = separator.shape[1] % (2 * W) == 0 and separator.shape[0] % W == 0
        if whole and row_panels.shape[1] % BLK == 0 and col_panels.shape[2] % BLK == 0 and mesh.shape["leaf"] == 2:
            return sparse_device(n_row, n_col, separator, col_panels, row_panels, *rest)
        return dense_device(separator, col_panels, row_panels, *rest)

    return jax.shard_map(
        per_device, mesh=mesh, in_specs=placed, out_specs=P("row", ("col", "leaf")), check_vma=False
    )
```

```python
import functools

import jax
import jax.numpy as jnp
from jax import lax
from jax.experimental import pallas as pl
from jax.experimental.pallas import tpu as pltpu
from jax.sharding import PartitionSpec as P

W = 256
BLK = 128
MESH = pl.DeviceIdType.MESH
PARTS = 2


def touched(index_list, positions):
    return jnp.any(index_list[:, :, :, None] == (positions // BLK)[None, None, None, :], axis=2)


def dense_device(separator, col_panels, row_panels, rows_list, cols_list, inverses):
    loc_rows = separator.shape[0]
    loc_cols = separator.shape[1]
    half = loc_cols // 2
    mine = lax.axis_index("leaf")
    row_ids = lax.axis_index("row") * loc_rows + jnp.arange(loc_rows, dtype=jnp.int32)
    subtrees = jnp.stack([mine])
    col_ids = lax.axis_index("col") * loc_cols + jnp.arange(loc_cols, dtype=jnp.int32)
    row_mask = touched(jnp.take(rows_list, subtrees, axis=0), row_ids)
    col_mask = touched(jnp.take(cols_list, subtrees, axis=0), col_ids)
    upper_all = lax.all_gather(row_panels, "row", axis=1, tiled=True)
    owner_all = jnp.arange(upper_all.shape[1], dtype=jnp.int32) // W
    keep_upper = jnp.take(col_mask, owner_all, axis=1)
    upper_all = jnp.where(keep_upper, upper_all, jnp.zeros_like(upper_all))
    piece = lax.all_gather(col_panels, "col", axis=2, tiled=True)
    owner = jnp.arange(piece.shape[2], dtype=jnp.int32) // W
    keep_lower = jnp.transpose(jnp.take(row_mask, owner, axis=1), (0, 2, 1))
    masked = jnp.where(keep_lower, piece, jnp.zeros_like(piece))
    update = jnp.einsum("srj,sjc->rc", masked, upper_all, preferred_element_type=jnp.float32)
    own_part = lax.dynamic_slice_in_dim(separator, mine * half, half, 1)
    both = lax.psum_scatter(update, "leaf", scatter_dimension=1, tiled=True)
    combined = own_part - both
    blocks = combined.reshape(loc_rows // W, W, half)
    factor = inverses.reshape(loc_rows // W, W, W)
    solved = jnp.einsum("bij,bjc->bic", factor, blocks, precision=lax.Precision.HIGHEST)
    return solved.reshape(loc_rows, half)


def pack_kernel(n_row, n_col, tr, tc, hb, nb, kk, caps_u, caps_l, tab, own, other, col, pu, pc, level):
    base_l = n_row * 2 * tr * hb
    base_i = base_l + 2 * n_col * tc * nb
    r, c, mine = tab[base_i], tab[base_i + 1], tab[base_i + 2]
    sw = W // BLK
    base_u, halves = base_i + 3, 2 * n_col
    base_r = base_u + 2 * kk * halves

    def most_in_rows(h, most):
        for x in range(n_row):
            parts = [tab[base_u + (leaf * kk + (x * tr + t) // sw) * halves + h] for leaf in range(2) for t in range(tr)]
            most = jnp.maximum(most, sum(parts[1:], parts[0]))
        return most

    def most_in_cols(h, most):
        for leaf in range(2):
            for x in range(n_col):
                parts = [tab[base_r + (leaf * kk + (x * tc + t) // sw) * n_row + h] for t in range(tc)]
                most = jnp.maximum(most, sum(parts[1:], parts[0]))
        return most

    most_u = lax.fori_loop(0, halves, most_in_rows, jnp.int32(0))
    most_l = lax.fori_loop(0, n_row, most_in_cols, jnp.int32(0))
    over = jnp.int32(0)
    for cap_u, cap_l in zip(caps_u[:-1], caps_l[:-1]):
        over = over + jnp.logical_or(most_u > cap_u, most_l > cap_l).astype(jnp.int32)
    level[0] = over

    for src, leaf in ((own, mine), (other, 1 - mine)):
        for t in range(tr):
            @pl.loop(0, hb)
            def _(j, src=src, leaf=leaf, t=t):
                p = tab[((r * 2 + leaf) * tr + t) * hb + j]

                @pl.when(p >= 0)
                def _():
                    at = pl.ds(pl.multiple_of(j * BLK, BLK), BLK)
                    pu[p] = src[0, pl.ds(t * BLK, BLK), at]
    for t in range(tc):
        @pl.loop(0, nb)
        def _(i, t=t):
            p = tab[base_l + ((mine * n_col + c) * tc + t) * nb + i]

            @pl.when(p >= 0)
            def _():
                at = pl.ds(pl.multiple_of(i * BLK, BLK), BLK)
                pc[p] = col[0, at, pl.ds(t * BLK, BLK)]


def comm_kernel(n_row, n_col, cap_u, cap_l, pu, pc, gu, gc, su, ru, sl, rl, sf, rf):
    r, c, mine = lax.axis_index("row"), lax.axis_index("col"), lax.axis_index("leaf")
    nu, nl = pl.ds(0, cap_u), pl.ds(0, cap_l)
    barrier = pltpu.get_barrier_semaphore()
    for d in (1, n_row - 1):
        pl.semaphore_signal(barrier, inc=1, device_id={"row": lax.rem(r + d, n_row)}, device_id_type=MESH)
    for d in range(1, n_col):
        pl.semaphore_signal(barrier, inc=1, device_id={"col": lax.rem(c + d, n_col)}, device_id_type=MESH)
    pl.semaphore_signal(barrier, inc=1, device_id={"leaf": 1 - mine}, device_id_type=MESH)
    pl.semaphore_wait(barrier, n_col + 2)

    cuts = [cap_u * x // PARTS for x in range(PARTS + 1)]

    def line(way, step, part, shard, target):
        piece = pl.ds(cuts[part], cuts[part + 1] - cuts[part])
        src = pu.at[piece] if step == 0 else gu.at[shard, piece]
        return pltpu.make_async_remote_copy(
            src_ref=src, dst_ref=gu.at[shard, piece], send_sem=su.at[way, step, part],
            recv_sem=ru.at[way, step, part], device_id={"row": target}, device_id_type=MESH)

    def line_send(way, step, part, act):
        goes = jnp.logical_and(r >= 1, r + step <= n_row - 1) if way == 0 else jnp.logical_and(r <= n_row - 2, r >= step)

        @pl.when(goes)
        def _():
            act(line(way, step, part, r + step if way == 0 else r - step, r - 1 if way == 0 else r + 1))

    def line_wait(way, step, part):
        @pl.when(r + 1 + step <= n_row - 1 if way == 0 else r >= 1 + step)
        def _():
            shard, source = (r + 1 + step, r + 1) if way == 0 else (r - 1 - step, r - 1)
            line(way, step, part, shard, source).wait_recv()

    def across(d):
        return pltpu.make_async_remote_copy(
            src_ref=pc.at[nl], dst_ref=gc.at[mine * n_col + c, nl], send_sem=sl.at[d], recv_sem=rl.at[d],
            device_id={"col": lax.rem(c + d, n_col)}, device_id_type=MESH)

    def arrived(d):
        slot = mine * n_col + lax.rem(c + n_col - d, n_col)
        return pltpu.make_async_remote_copy(
            src_ref=pc.at[nl], dst_ref=gc.at[slot, nl], send_sem=sl.at[d], recv_sem=rl.at[d],
            device_id={"col": lax.rem(c + d, n_col)}, device_id_type=MESH)

    def pair(d, leaf):
        slot = leaf * n_col + lax.rem(c + n_col - d, n_col)
        return pltpu.make_async_remote_copy(
            src_ref=pc.at[nl] if d == 0 else gc.at[slot, nl], dst_ref=gc.at[slot, nl],
            send_sem=sf.at[d], recv_sem=rf.at[d], device_id={"leaf": 1 - mine}, device_id_type=MESH)

    for part in range(PARTS):
        for way in range(2):
            line_send(way, 0, part, lambda copy: copy.start())
    for d in range(1, n_col):
        across(d).start()
    pair(0, mine).start()
    for step in range(n_row - 1):
        for part in range(PARTS):
            for way in range(2):
                line_wait(way, step, part)
                if step < n_row - 2:
                    line_send(way, step + 1, part, lambda copy: copy.start())
        if step == 0:
            for d in range(1, n_col):
                arrived(d).wait_recv()
                pair(d, mine).start()
    for d in range(n_col):
        pair(d, 1 - mine).wait_recv()
    for d in range(n_col):
        pair(d, mine).wait_send()
    for d in range(1, n_col):
        across(d).wait_send()
    for step in range(n_row - 1):
        for part in range(PARTS):
            for way in range(2):
                line_send(way, step, part, lambda copy: copy.wait_send())


def split(x):
    hi = x.astype(jnp.bfloat16)
    return hi, (x - hi.astype(jnp.float32)).astype(jnp.bfloat16)


GROUP = 4


def solve_kernel(n_row, n_col, tr, tc, hb, nb, kk, tab, sep, inv, pu, pc, gu, gc, out,
                 low, up, acc, prod, row_at, col_at, sem, sep_sem):
    base_l = n_row * 2 * tr * hb
    base_i = base_l + 2 * n_col * tc * nb
    sw = W // BLK
    half, loc_rows = hb * BLK, nb * BLK
    b = pl.program_id(0)

    def at_u(leaf, k, q):
        s = k * sw + q
        return (((s // tr) * 2 + leaf) * tr + s % tr) * hb

    def at_l(leaf, k, q):
        return base_l + (leaf * kk * sw + k * sw + q) * nb

    @pl.when(b == 0)
    def _():
        r, c, mine = tab[base_i], tab[base_i + 1], tab[base_i + 2]
        load = pltpu.make_async_copy(
            sep.at[:, pl.ds(pl.multiple_of(mine * half, half), half)],
            acc.at[pl.ds(0, loc_rows), pl.ds(0, half)], sep_sem)
        load.start()
        counts = []
        total = jnp.int32(0)
        for leaf in range(2):
            for k in range(kk):
                m = leaf * kk + k

                def take_col(j, n, leaf=leaf, k=k, m=m):
                    hit = tab[at_u(leaf, k, 0) + j] >= 0

                    @pl.when(hit)
                    def _():
                        col_at[m * (hb + GROUP) + n] = j
                        at = pl.ds(pl.multiple_of(n * BLK, BLK), BLK)
                        for q in range(sw):
                            p = tab[at_u(leaf, k, q) + j]
                            owner = (k * sw + q) // tr
                            dst = up.at[m, pl.ds(q * BLK, BLK), at]

                            @pl.when(owner == r)
                            def _():
                                pltpu.make_async_copy(pu.at[p], dst, sem).start()

                            @pl.when(owner != r)
                            def _():
                                pltpu.make_async_copy(gu.at[owner, p], dst, sem).start()
                    return n + hit.astype(jnp.int32)

                def take_row(i, n, leaf=leaf, k=k, m=m):
                    hit = tab[at_l(leaf, k, 0) + i] >= 0

                    @pl.when(hit)
                    def _():
                        row_at[m * (nb + GROUP) + n] = i
                        at = pl.ds(pl.multiple_of(n * BLK, BLK), BLK)
                        for q in range(sw):
                            p = tab[at_l(leaf, k, q) + i]
                            owner = (k * sw + q) // tc
                            here = jnp.logical_and(owner == c, leaf == mine)
                            dst = low.at[m, at, pl.ds(q * BLK, BLK)]

                            @pl.when(here)
                            def _():
                                pltpu.make_async_copy(pc.at[p], dst, sem).start()

                            @pl.when(jnp.logical_not(here))
                            def _():
                                pltpu.make_async_copy(gc.at[leaf * n_col + owner, p], dst, sem).start()
                    return n + hit.astype(jnp.int32)

                n_u = lax.fori_loop(0, hb, take_col, jnp.int32(0))
                n_l = lax.fori_loop(0, nb, take_row, jnp.int32(0))
                for e in range(GROUP):
                    col_at[m * (hb + GROUP) + n_u + e] = jnp.int32(hb)
                    row_at[m * (nb + GROUP) + n_l + e] = jnp.int32(nb)
                counts.append((n_u, n_l))
                total = total + (n_u + n_l) * sw

        @pl.loop(0, total)
        def _(n):
            pltpu.make_async_copy(pc.at[0], low.at[0, pl.ds(0, BLK), pl.ds(0, BLK)], sem).wait()

        load.wait()
        wide = GROUP * BLK
        for m, (n_u, n_l) in enumerate(counts):
            @pl.loop(0, (n_l + GROUP - 1) // GROUP)
            def _(x, m=m, n_u=n_u, n_l=n_l):
                rows = pl.ds(pl.multiple_of(x * wide, wide), wide)

                @pl.loop(0, (n_u + GROUP - 1) // GROUP)
                def _(y):
                    cols = pl.ds(pl.multiple_of(y * wide, wide), wide)
                    prod[...] = jnp.dot(low[m, rows, :], up[m, :, cols], preferred_element_type=jnp.float32)
                    for i in range(GROUP):
                        row = row_at[m * (nb + GROUP) + x * GROUP + i]

                        @pl.when(row < nb)
                        def _(i=i, row=row):
                            to = pl.ds(pl.multiple_of(row * BLK, BLK), BLK)
                            for j in range(GROUP):
                                col = col_at[m * (hb + GROUP) + y * GROUP + j]
                                at = pl.ds(pl.multiple_of(col * BLK, BLK), BLK)
                                acc[to, at] -= prod[i * BLK:(i + 1) * BLK, j * BLK:(j + 1) * BLK]

    tile = min(512, half)
    rows = pl.ds(pl.multiple_of(b * W, W), W)
    f_hi, f_lo = split(inv[...])
    for n in range(half // tile):
        at = pl.ds(n * tile, tile)
        hi, lo = split(acc[rows, at])
        out[:, at] = (jnp.dot(f_hi, hi, preferred_element_type=jnp.float32)
                      + (jnp.dot(f_hi, lo, preferred_element_type=jnp.float32)
                         + jnp.dot(f_lo, hi, preferred_element_type=jnp.float32)))


def solve_call(n_row, n_col, tr, tc, hb, nb, kk):
    hbm = pl.BlockSpec(memory_space=pl.ANY)
    half, loc_rows = hb * BLK, nb * BLK
    hg, ng = -(-hb // GROUP) * GROUP, -(-nb // GROUP) * GROUP
    return pl.pallas_call(
        functools.partial(solve_kernel, n_row, n_col, tr, tc, hb, nb, kk),
        out_shape=jax.ShapeDtypeStruct((loc_rows, half), jnp.float32),
        grid_spec=pltpu.PrefetchScalarGridSpec(
            num_scalar_prefetch=1, grid=(loc_rows // W,),
            in_specs=[hbm, pl.BlockSpec((W, W), lambda i, t: (i, 0)), hbm, hbm, hbm, hbm],
            out_specs=pl.BlockSpec((W, half), lambda i, t: (i, 0)),
            scratch_shapes=[pltpu.VMEM((2 * kk, ng * BLK, W), jnp.bfloat16),
                            pltpu.VMEM((2 * kk, W, hg * BLK), jnp.bfloat16),
                            pltpu.VMEM((loc_rows, half + BLK), jnp.float32),
                            pltpu.VMEM((GROUP * BLK, GROUP * BLK), jnp.float32),
                            pltpu.SMEM((2 * kk * (nb + GROUP),), jnp.int32),
                            pltpu.SMEM((2 * kk * (hb + GROUP),), jnp.int32),
                            pltpu.SemaphoreType.DMA, pltpu.SemaphoreType.DMA]),
        compiler_params=pltpu.CompilerParams(vmem_limit_bytes=58 * 2**20),
    )


def caps(full, fractions):
    return [max(1, -(-full * f // 96)) for f in fractions] + [full]


def sparse_device(n_row, n_col, separator, col_panels, row_panels, rows_list, cols_list, inverses):
    loc_rows, loc_cols = separator.shape
    half = loc_cols // 2
    tr, tc = row_panels.shape[1] // BLK, col_panels.shape[2] // BLK
    hb, nb = half // BLK, loc_rows // BLK
    kk = rows_list.shape[1]
    sw = W // BLK
    full_u, full_l = 2 * tr * hb, tc * nb
    r, c, mine = lax.axis_index("row"), lax.axis_index("col"), lax.axis_index("leaf")

    away = lax.dynamic_slice_in_dim(row_panels, (1 - mine) * half, half, 2)
    other = lax.ppermute(away, "leaf", [(0, 1), (1, 0)])

    def slices(mask, lead):
        return jnp.broadcast_to(mask[:, :, None], (2, kk, sw) + mask.shape[2:]).reshape((2, lead, -1) + mask.shape[2:])

    def places(mask):
        n = mask.shape[1]
        before = (jnp.arange(n)[:, None] < jnp.arange(n)[None, :]).astype(jnp.bfloat16)
        at = jnp.dot(mask.astype(jnp.bfloat16), before, preferred_element_type=jnp.float32).astype(jnp.int32)
        return jnp.where(mask, at, -1).reshape(-1)

    def named(index_list, ids):
        return jnp.any(index_list[:, :, :, None] == ids, axis=2)

    mine_u = named(cols_list, (c * 2 + mine) * hb + jnp.arange(hb, dtype=jnp.int32))
    mine_u = jnp.transpose(slices(mine_u, n_row), (1, 0, 2, 3)).reshape(n_row, full_u)
    mine_l = named(rows_list, r * nb + jnp.arange(nb, dtype=jnp.int32))
    mine_l = slices(mine_l, n_col).reshape(2 * n_col, full_l)
    all_u = named(cols_list, jnp.arange(n_col * 2 * hb, dtype=jnp.int32)).reshape(2, kk, n_col * 2, hb)
    all_l = named(rows_list, jnp.arange(n_row * nb, dtype=jnp.int32)).reshape(2, kk, n_row, nb)
    tab = jnp.concatenate([
        places(mine_u), places(mine_l), jnp.stack([r, c, mine]).astype(jnp.int32),
        jnp.sum(all_u, axis=3, dtype=jnp.int32).reshape(-1), jnp.sum(all_l, axis=3, dtype=jnp.int32).reshape(-1)])
    caps_u = caps(full_u, (24, 26, 28, 30, 32, 34, 36, 40, 48))
    caps_l = caps(full_l, (40, 44, 44, 44, 48, 48, 48, 52, 60))

    block = (BLK, BLK)
    bf16 = jnp.bfloat16
    at_leaf = n_row * full_u + 2 * n_col * full_l + 2
    pu, pc, level = pl.pallas_call(
        functools.partial(pack_kernel, n_row, n_col, tr, tc, hb, nb, kk, caps_u, caps_l),
        out_shape=(jax.ShapeDtypeStruct((full_u,) + block, bf16), jax.ShapeDtypeStruct((full_l,) + block, bf16),
                   jax.ShapeDtypeStruct((1,), jnp.int32)),
        grid_spec=pltpu.PrefetchScalarGridSpec(
            num_scalar_prefetch=1, grid=(1,),
            in_specs=[
                pl.BlockSpec((1, tr * BLK, half), lambda i, t: (0, 0, t[at_leaf])),
                pl.BlockSpec((1, tr * BLK, half), lambda i, t: (0, 0, 0)),
                pl.BlockSpec((1, loc_rows, tc * BLK), lambda i, t: (0, 0, 0)),
            ],
            out_specs=[pl.BlockSpec((full_u,) + block, lambda i, t: (0, 0, 0)),
                       pl.BlockSpec((full_l,) + block, lambda i, t: (0, 0, 0)),
                       pl.BlockSpec(memory_space=pltpu.SMEM)]),
        compiler_params=pltpu.CompilerParams(vmem_limit_bytes=60 * 2**20),
    )(tab, row_panels, other, col_panels)

    hbm = pl.BlockSpec(memory_space=pl.ANY)
    dma = pltpu.SemaphoreType.DMA

    def exchange(which):
        def run(a, b):
            return pl.pallas_call(
                functools.partial(comm_kernel, n_row, n_col, caps_u[which], caps_l[which]),
                out_shape=(jax.ShapeDtypeStruct((n_row, full_u) + block, bf16),
                           jax.ShapeDtypeStruct((2 * n_col, full_l) + block, bf16)),
                in_specs=[hbm, hbm], out_specs=(hbm, hbm),
                scratch_shapes=[dma((2, n_row, PARTS)), dma((2, n_row, PARTS))] + [dma((n_col,))] * 4,
                compiler_params=pltpu.CompilerParams(collective_id=which, has_side_effects=True),
                name="exchange%d" % which,
            )(a, b)
        return run

    gu, gc = lax.switch(level[0], [exchange(i) for i in range(len(caps_u))], pu, pc)

    solve = solve_call(n_row, n_col, tr, tc, hb, nb, kk)
    return solve(tab, separator, inverses, pu, pc, gu, gc)


def solution(mesh):
    placed = (
        P("row", "col"),
        P("leaf", "row", "col"),
        P("leaf", "row", "col"),
        P(),
        P(),
        P("row", None),
    )
    n_row, n_col = mesh.shape["row"], mesh.shape["col"]

    def per_device(separator, col_panels, row_panels, *rest):
        whole = separator.shape[1] % (2 * W) == 0 and separator.shape[0] % W == 0
        if whole and row_panels.shape[1] % BLK == 0 and col_panels.shape[2] % BLK == 0 and mesh.shape["leaf"] == 2:
            return sparse_device(n_row, n_col, separator, col_panels, row_panels, *rest)
        return dense_device(separator, col_panels, row_panels, *rest)

    return jax.shard_map(
        per_device, mesh=mesh, in_specs=placed, out_specs=P("row", ("col", "leaf")), check_vma=False
    )
```
